32 devices in a mesh: row: 4 (over z), col: 8 (over y, x, core).
Axes of the slice: x: 2, y: 2, z: 4, core: 2. Of those that a mesh axis runs over, the one named last changes fastest.
Arguments:
- load_amp: float32 [2048, 4096], P('row', 'col'), may hold values from 0.05 to 1
- load_mask: int32 [2048, 4096], P('row', 'col'), may hold values 0 or 1
- leak: float32 [2048, 4096], P('row', 'col'), may hold values from 0.001 to 0.05
- coarse_leak: float32 [512, 1024], P('row', 'col'), may hold values from 0.01 to 0.5
- coarse_init: float32 [512, 1024], P('row', 'col'), may hold values from 0 to 1
- via_fine: int32 [4, 8192], P('row', 'col'), may hold values from 0 to 262143
- via_coarse: int32 [4, 8192], P('row', 'col'), may hold values from 0 to 131071, as said below
- via_count: int32 [4, 64], P('row', 'col'), may hold values from 0 to 128, as said below
Outputs:
- fine_drop: float32 [2048, 4096], P('row', 'col')
- coarse_drop: float32 [512, 1024], P('row', 'col')
The draws below stay inside these ranges and needn't reach their ends.
Inputs may be any that keep to these rules, and one draw needn't show every extreme that they name: `via_coarse`: slot s of a tile names a coarse node whose stored column lies in s // 128 * 128 to s // 128 * 128 + 127. `via_count`: slots of an owner past its count are padding and carry arbitrary indices. In each tile row some owner gets 128 live slots from every tile of that row.
All inputs are finite; a program needn't handle non-finite values. No bound on the sum of `load_mask` on one device may be relied on, other than what follows from the above.
Results may differ from the reference program's by a relative error of at most 0.00022.
Values sent between devices are 32-bit elements; how exact they have to be, the bound alone decides.
A program may use at most 64 MiB of HBM per device.

```python
import math
import jax
import jax.numpy as jnp

FR = 512
FC = 512
CR = 128
CC = 128
GROUP = 16
VOWN = 128
ITERS = 4
OUTER = 1
CSWEEP = 2
NFR = 2048
NFC = 4096
NCR = 512
NCC = 1024
VMAX = 1024
N_ROW = 4
N_COL = 8


def draw_via_coarse(key, part):
    columns = NCC // CC
    tiles_down = NCR // CR
    slot_all = jnp.arange(columns * VMAX, dtype=jnp.int32)
    owner = slot_all % VMAX // VOWN
    key_row, key_col = jax.random.split(jax.random.fold_in(key, 11))
    shape = (tiles_down, columns * VMAX)
    row_pick = jax.random.randint(key_row, shape, 0, CR, dtype=jnp.int32)
    col_pick = jax.random.randint(key_col, shape, 0, CC, dtype=jnp.int32)
    return (row_pick * NCC + owner[None, :] * CC + col_pick).astype(jnp.int32)


def draw_via_count(key, part):
    columns = NCC // CC
    tiles_down = NCR // CR
    key_base, key_full = jax.random.split(jax.random.fold_in(key, 23))
    base = jax.random.randint(key_base, (tiles_down, columns * columns), 0, VOWN + 1, dtype=jnp.int32)
    chosen = jax.random.randint(key_full, (tiles_down, 1), 0, columns, dtype=jnp.int32)
    owner = jnp.arange(columns * columns, dtype=jnp.int32) % columns
    return jnp.where(owner[None, :] == chosen, VOWN, base).astype(jnp.int32)


def touch_ends(array, stream_key, low, high):
    shape = array.shape
    place = [jax.random.randint(jax.random.fold_in(stream_key, axis), (), 0, shape[axis]) for axis in range(len(shape))]
    array = array.at[tuple(place)].set(low)
    longest = shape.index(max(shape))
    place[longest] = (place[longest] + 1) % shape[longest]
    return array.at[tuple(place)].set(high)


def levels(own_key, dims, cuts, low, top_value):
    level, own = 1.0, jax.random.fold_in(own_key, 6)
    for dim, blocks in cuts:
        draws = jnp.exp(jax.random.uniform(jax.random.fold_in(own, dim), (blocks,), jnp.float32, low / len(cuts), top_value / len(cuts)))
        level = level * jnp.repeat(draws, dims[dim] // blocks).reshape([-1 if axis == dim else 1 for axis in range(len(dims))])
    return level


def setup_inputs(seed: int = 0) -> dict:
    key_of = jax.random.split(jax.random.key(seed), 9)
    load_amp = jnp.clip(jnp.exp(math.log(1.0) - 2.9957323 * jax.random.uniform(key_of[0], (NFR, NFC), jnp.float32) ** levels(key_of[0], (NFR, NFC), ((0, 4), (1, 8)), -0.2, 0.2)), 0.05, 1.0)
    load_mask = touch_ends((jax.random.randint(key_of[1], (NFR, NFC), 0, 2) < 1).astype(jnp.int32), jax.random.fold_in(key_of[1], 1), 0, 1)
    leak = jnp.clip(jnp.exp(math.log(0.05) - 3.912023 * jax.random.uniform(key_of[2], (NFR, NFC), jnp.float32) ** levels(key_of[2], (NFR, NFC), ((0, 4), (1, 8)), -0.2, 0.2)), 0.001, 0.05)
    coarse_leak = jnp.clip(jnp.exp(math.log(0.5) - 3.912023 * jax.random.uniform(key_of[3], (NCR, NCC), jnp.float32) ** levels(key_of[3], (NCR, NCC), ((0, 4), (1, 8)), -0.2, 0.2)), 0.01, 0.5)
    coarse_init = jnp.clip(1.0 * jax.random.uniform(key_of[4], (NCR, NCC), jnp.float32) ** levels(key_of[4], (NCR, NCC), ((0, 4), (1, 8)), -0.2, 0.2), 0.0, 1.0)
    via_fine = touch_ends(jax.random.randint(key_of[5], (N_ROW, VMAX * N_COL), 0, FR * FC), jax.random.fold_in(key_of[5], 1), 0, (FR * FC) - 1).astype(jnp.int32)
    via_coarse = draw_via_coarse(jax.random.fold_in(key_of[8], 71), 0)
    via_count = draw_via_count(jax.random.fold_in(key_of[8], 71), 0)
    return {"load_amp": load_amp, "load_mask": load_mask, "leak": leak, "coarse_leak": coarse_leak, "coarse_init": coarse_init, "via_fine": via_fine, "via_coarse": via_coarse, "via_count": via_count}


via_conductance = 2.0
coarse_conductance = 4.0
relaxation = 0.8


def fine_apply(field, diagonal):
    padded = jnp.pad(field, 1)
    beside = padded[2:, 1:-1] + padded[:-2, 1:-1] + padded[1:-1, 2:] + padded[1:-1, :-2]
    return diagonal * field - beside


def to_physical(stored):
    return stored.reshape(NCR, N_COL, CC // GROUP, GROUP).transpose(0, 2, 1, 3).reshape(NCR, NCC)


def to_stored(physical):
    return physical.reshape(NCR, CC // GROUP, N_COL, GROUP).transpose(0, 2, 1, 3).reshape(NCR, NCC)


def coarse_apply(stored, diagonal):
    padded = jnp.pad(to_physical(stored), 1)
    beside = padded[2:, 1:-1] + padded[:-2, 1:-1] + padded[1:-1, 2:] + padded[1:-1, :-2]
    return diagonal * stored - coarse_conductance * to_stored(beside)


def reference(load_amp, load_mask, leak, coarse_leak, coarse_init, via_fine, via_coarse, via_count):
    tile_row = jnp.arange(N_ROW, dtype=jnp.int32)[:, None]
    slot_all = jnp.arange(N_COL * VMAX, dtype=jnp.int32)[None, :]
    tile_col = slot_all // VMAX
    within = slot_all % VMAX
    owner = within // VOWN
    position = within % VOWN
    count_index = jnp.broadcast_to(tile_col * N_COL + owner, via_fine.shape).astype(jnp.int32)
    counts = jnp.take_along_axis(via_count, count_index, axis=1)
    weight = jnp.where(position < counts, via_conductance, 0.0).astype(jnp.float32).reshape(-1)
    fine_index = ((tile_row * FR + via_fine // FC) * NFC + tile_col * FC + via_fine % FC).reshape(-1)
    coarse_index = ((tile_row * CR + via_coarse // NCC) * NCC + via_coarse % NCC).reshape(-1)
    fine_diag = 4.0 + leak + jnp.zeros(NFR * NFC, jnp.float32).at[fine_index].add(weight).reshape(NFR, NFC)
    coarse_diag = 4.0 * coarse_conductance + coarse_leak + jnp.zeros(NCR * NCC, jnp.float32).at[coarse_index].add(weight).reshape(NCR, NCC)
    load = load_amp * load_mask.astype(jnp.float32)
    volt = coarse_init
    solution = jnp.zeros((NFR, NFC), jnp.float32)
    for outer_turn in range(OUTER):
        at_via = volt.reshape(-1)[coarse_index]
        rhs = load + jnp.zeros(NFR * NFC, jnp.float32).at[fine_index].add(weight * at_via).reshape(NFR, NFC)
        residual = rhs - fine_apply(solution, fine_diag)
        precond = residual / fine_diag
        direction = precond
        product = jnp.sum(residual * precond)
        for iteration in range(ITERS):
            image = fine_apply(direction, fine_diag)
            alpha = product / jnp.sum(direction * image)
            solution = solution + alpha * direction
            residual = residual - alpha * image
            if iteration + 1 < ITERS:
                precond = residual / fine_diag
                renewed = jnp.sum(residual * precond)
                direction = precond + (renewed / product) * direction
                product = renewed
        at_fine = weight * solution.reshape(-1)[fine_index]
        sources = jnp.zeros(NCR * NCC, jnp.float32).at[coarse_index].add(at_fine).reshape(NCR, NCC)
        for sweep_turn in range(CSWEEP):
            volt = volt + relaxation * (sources - coarse_apply(volt, coarse_diag)) / coarse_diag
    return solution, volt
```

```python
import functools
import jax
import jax.numpy as jnp
from jax import lax
from jax.experimental import pallas as pl
from jax.experimental.pallas import tpu as pltpu
from jax.sharding import PartitionSpec as P

GROUP = 16
ITERS = 4
LANES = 128

via_conductance = 2.0
coarse_conductance = 4.0
relaxation = 0.8

F32 = jnp.float32
BF16 = jnp.bfloat16


def divide(value, by):
    if by & (by - 1) == 0:
        return lax.shift_right_logical(value, by.bit_length() - 1)
    return value // by


def remainder(value, by):
    if by & (by - 1) == 0:
        return value & (by - 1)
    return value % by


def halves(value):
    high = value.astype(BF16).astype(F32)
    return high, value - high


def dot(a, b):
    return jnp.dot(a, b, preferred_element_type=F32)


def chunk_of(rows, top):
    size = top
    while rows % size:
        size -= 8
    return size


def kernel(
    R, C,
    amp, mask, leak, cleak, cinit, vf, vc, cnt,
    x_out, c_out,
    msg_out, msg_in, val_out, val_in, fval_out, fval_in,
    B, Bt, dv, V, Y, rhs,
    E, ET, H, rtop, rbot, rcorner,
    red_out, red_in, red2_out, red2_in,
    volt1, crow_top, crow_bot, cleft, cright,
    send_sem, recv_sem,
):
    row, col = lax.axis_index("row"), lax.axis_index("col")
    TR, TC = leak.shape
    BR, BC = cleak.shape
    S = vf.shape[1]
    per = S // C
    up, down = lax.rem(row + R - 1, R), lax.rem(row + 1, R)
    left, right = lax.rem(col + C - 1, C), lax.rem(col + 1, C)

    barrier = pltpu.get_barrier_semaphore()
    peers = [(row, lax.rem(col + d, C)) for d in range(1, C)]
    peers += [(lax.rem(row + d, R), col) for d in range(1, R)]
    peers += [(u, s) for u in (up, down) for s in (left, right)]
    for peer in peers:
        pl.semaphore_signal(barrier, inc=1, device_id=peer, device_id_type=pl.DeviceIdType.MESH)

    count = [0]
    pending = []

    def send(src, dst, device):
        n = count[0]
        count[0] += 1
        copy = pltpu.make_async_remote_copy(
            src_ref=src, dst_ref=dst, send_sem=send_sem.at[n], recv_sem=recv_sem.at[n],
            device_id=device, device_id_type=pl.DeviceIdType.MESH,
        )
        copy.start()
        pending.append(copy)
        return copy

    lane = lax.broadcasted_iota(jnp.int32, (1, per), 1)
    weight = jnp.concatenate(
        [jnp.where(lane < cnt[0, o], via_conductance, 0.0).astype(F32) for o in range(C)], axis=1
    )
    node = vc[...]
    node_row = divide(node, BC * C).astype(F32)
    node_col = remainder(node, BC).astype(F32)
    for o in range(C):
        cut = slice(o * per, (o + 1) * per)
        msg_out[o, 0:1, :] = node_row[:, cut]
        msg_out[o, 1:2, :] = node_col[:, cut]
        msg_out[o, 2:3, :] = weight[:, cut]
        msg_out[o, 3:8, :] = jnp.zeros((5, per), F32)
    msg_in[col] = msg_out[col]
    for n in range(2):
        H[n] = jnp.zeros((LANES, TR), F32)
    pl.semaphore_wait(barrier, len(peers))

    messages = [
        send(msg_out.at[lax.rem(col + d, C)], msg_in.at[col], (row, lax.rem(col + d, C)))
        for d in range(1, C)
    ]

    def coarse_send(ref, n):
        return [
            send(ref.at[pl.ds(0, 8)], crow_bot.at[n], (up, col)),
            send(ref.at[pl.ds(BR - 8, 8)], crow_top.at[n], (down, col)),
            send(ref, cright.at[n], (row, left)),
            send(ref, cleft.at[n], (row, right)),
        ]

    coarse0 = coarse_send(cinit, 0)

    fine = vf[...]
    fine_row = divide(fine, TC)
    fine_col = remainder(fine, TC)
    step = 64

    def build_cols(i, carry):
        at = pl.ds(pl.multiple_of(i * step, step), step)
        place = lax.broadcasted_iota(jnp.int32, (step, S), 0) + i * step
        B[at, :] = jnp.where(place == fine_col, 1.0, 0.0).astype(BF16)
        return carry

    lax.fori_loop(0, TC // step, build_cols, 0)
    lanes = lax.broadcasted_iota(jnp.int32, (per, TC), 1).astype(F32)
    for o in range(C):
        cut = slice(o * per, (o + 1) * per)
        turned = jnp.broadcast_to(fine_col[:, cut].astype(F32), (LANES, per)).T
        wide = jnp.concatenate([turned] * (TC // LANES), axis=1)
        Bt[cut, :] = jnp.where(wide == lanes, 1.0, 0.0).astype(BF16)

    zero_pad = jnp.zeros((8, TC + LANES), F32)
    for n in range(ITERS):
        V[n, 0:8, :] = zero_pad
        V[n, TR + 24 : TR + 32, :] = zero_pad

    def diagonal(i, carry):
        at = pl.ds(pl.multiple_of(i * step, step), step)
        inner = pl.ds(pl.multiple_of(16 + i * step, 8), step)
        place = lax.broadcasted_iota(jnp.int32, (step, S), 0) + i * step
        match = place == fine_row
        value = 4.0 + leak[at, :] + dot(jnp.where(match, weight, 0.0).astype(BF16), Bt[...])
        dv[inner, 0:TC] = 1.0 / value
        return carry

    lax.fori_loop(0, TR // step, diagonal, 0)

    low_side = lax.broadcasted_iota(jnp.int32, (TR, LANES), 1) < LANES // 2

    def halo_send(F, n):
        edge = jnp.where(low_side, F[16 : 16 + TR, 0:LANES], F[16 : 16 + TR, TC - LANES : TC])
        E[n] = edge
        ET[n] = edge.T
        return [
            send(F.at[pl.ds(16, 8), pl.ds(0, TC)], rbot.at[n], (up, col)),
            send(F.at[pl.ds(TR + 8, 8), pl.ds(0, TC)], rtop.at[n], (down, col)),
            send(ET.at[n, pl.ds(0, 8)], H.at[n, pl.ds(0, 8)], (row, left)),
            send(ET.at[n, pl.ds(LANES - 8, 8)], H.at[n, pl.ds(LANES - 8, 8)], (row, right)),
            send(E.at[n, pl.ds(0, 8)], rcorner.at[n, 3], (up, left)),
            send(E.at[n, pl.ds(0, 8)], rcorner.at[n, 2], (up, right)),
            send(E.at[n, pl.ds(TR - 8, 8)], rcorner.at[n, 1], (down, left)),
            send(E.at[n, pl.ds(TR - 8, 8)], rcorner.at[n, 0], (down, right)),
        ]

    top_ok, bot_ok = row > 0, row < R - 1
    left_ok, right_ok = col > 0, col < C - 1

    def keep(ok, value):
        return value * jnp.where(ok, 1.0, 0.0).astype(F32)

    def halo_land(F, n, copies):
        for copy in copies:
            copy.wait_recv()
        F[8:16, 0:TC] = keep(top_ok, rtop[n])
        F[TR + 16 : TR + 24, 0:TC] = keep(bot_ok, rbot[n])
        side = H[n].T
        F[16 : 16 + TR, TC : TC + LANES] = jnp.where(
            low_side, keep(right_ok, side), keep(left_ok, side)
        )
        low8 = lax.broadcasted_iota(jnp.int32, (8, LANES), 1)
        near_low, near_high = low8 < 8, low8 >= LANES - 8

        def corner(ok, lo, hi):
            return keep(
                ok,
                jnp.where(near_low, keep(right_ok, lo), 0.0)
                + jnp.where(near_high, keep(left_ok, hi), 0.0),
            )

        F[8:16, TC : TC + LANES] = corner(top_ok, rcorner[n, 1], rcorner[n, 0])
        F[TR + 16 : TR + 24, TC : TC + LANES] = corner(bot_ok, rcorner[n, 3], rcorner[n, 2])

    for copy in messages:
        copy.wait_recv()
    heard = [msg_in[t] for t in range(C)]
    in_row = jnp.concatenate([m[0:1] for m in heard], axis=1).astype(jnp.int32)
    in_col = jnp.concatenate([m[1:2] for m in heard], axis=1).astype(jnp.int32)
    in_weight = jnp.concatenate([m[2:3] for m in heard], axis=1)
    place_r = lax.broadcasted_iota(jnp.int32, (BR, S), 0)
    place_c = lax.broadcasted_iota(jnp.int32, (BC, S), 0)
    row_hit = place_r == in_row
    col_hot = jnp.where(place_c == in_col, 1.0, 0.0).astype(BF16)
    hi, lo = halves(cinit[...])
    seen = dot(hi.astype(BF16), col_hot) + dot(lo.astype(BF16), col_hot)
    at_via = jnp.sum(jnp.where(row_hit, seen, 0.0), axis=0, keepdims=True)
    for t in range(C):
        val_out[t] = at_via[:, t * per : (t + 1) * per]
    val_in[col] = val_out[col]
    values = [
        send(val_out.at[lax.rem(col + d, C)], val_in.at[col], (row, lax.rem(col + d, C)))
        for d in range(1, C)
    ]

    dinv_copies = halo_send(dv, 0)

    def onto_coarse(amount):
        spread = jnp.where(row_hit, amount, 0.0).astype(BF16)
        return lax.dot_general(spread, col_hot, (((1,), (1,)), ((), ())), preferred_element_type=F32)

    coarse_diag = 4.0 * coarse_conductance + cleak[...] + onto_coarse(in_weight)

    for copy in values:
        copy.wait_recv()
    drops = weight * jnp.concatenate([val_in[o] for o in range(C)], axis=1)
    drop_hi, drop_lo = halves(drops)

    def inject(i, carry):
        at = pl.ds(pl.multiple_of(i * step, step), step)
        inner = pl.ds(pl.multiple_of(16 + i * step, 8), step)
        place = lax.broadcasted_iota(jnp.int32, (step, S), 0) + i * step
        match = place == fine_row
        added = dot(jnp.where(match, drop_hi, 0.0).astype(BF16), Bt[...])
        added += dot(jnp.where(match, drop_lo, 0.0).astype(BF16), Bt[...])
        value = amp[at, :] * mask[at, :].astype(F32) + added
        rhs[at, :] = value
        V[0, inner, 0:TC] = value * dv[inner, 0:TC]
        return carry

    lax.fori_loop(0, TR // step, inject, 0)
    first_copies = halo_send(V.at[0], 1)
    halo_land(dv, 0, dinv_copies)
    halo_land(V.at[0], 1, first_copies)

    rows = chunk_of(TR + 16, 48)
    width = TC + LANES

    def around(k, start, size):
        tall = V[k, pl.ds(pl.multiple_of(start - 8, 8), size + 16), :]
        mid = tall[8 : 8 + size]
        total = pltpu.roll(tall, 1, 0)[8 : 8 + size] + pltpu.roll(tall, size + 15, 0)[8 : 8 + size]
        return total + pltpu.roll(mid, 1, 1) + pltpu.roll(mid, width - 1, 1)

    for k in range(ITERS - 1):

        def advance(i, carry, k=k):
            start = pl.multiple_of(8 + i * rows, 8)
            near = around(k, start, rows)
            Y[k, pl.ds(start, rows), :] = near
            fresh = dv[pl.ds(start, rows), :] * near
            if k:
                fresh = 2.0 * fresh - V[k - 1, pl.ds(start, rows), :]
            V[k + 1, pl.ds(start, rows), :] = fresh
            return carry

        lax.fori_loop(0, (TR + 16) // rows, advance, 0)

    pairs = [(j, k) for k in range(ITERS) for j in range(k + 1)]
    sums = len(pairs) + ITERS

    def fold(value):
        total = value[:, 0:LANES]
        for n in range(1, TC // LANES):
            total = total + value[:, n * LANES : (n + 1) * LANES]
        return total

    def gram(i, carry):
        at = pl.ds(pl.multiple_of(i * 8, 8), 8)
        start = pl.multiple_of(16 + i * 8, 8)
        inner = pl.ds(start, 8)
        v = [V[k, inner, 0:TC] for k in range(ITERS)]
        y = [Y[k, inner, 0:TC] for k in range(ITERS - 1)]
        y.append(around(ITERS - 1, start, 8)[:, 0:TC])
        w = [rhs[at, :], y[0]]
        for k in range(2, ITERS):
            w.append(2.0 * y[k - 1] - w[k - 2])
        applied = [w[k] - y[k] for k in range(ITERS)]
        fresh = [fold(v[j] * applied[k]) for j, k in pairs] + [fold(w[0] * v[k]) for k in range(ITERS)]
        return tuple(a + b for a, b in zip(carry, fresh))

    totals = lax.fori_loop(0, TR // 8, gram, tuple(jnp.zeros((8, LANES), F32) for _ in range(sums)))
    red_out[...] = jnp.zeros(red_out.shape, F32)
    for n, total in enumerate(totals):
        red_out[n : n + 1, :] = jnp.sum(total, axis=0, keepdims=True)
    copies = [
        send(red_out, red_in.at[d - 1], (row, lax.rem(col + d, C))) for d in range(1, C)
    ]
    total = red_out[...]
    for d, copy in enumerate(copies):
        copy.wait_recv()
        total = total + red_in[d]
    red2_out[...] = total
    copies = [
        send(red2_out, red2_in.at[d - 1], (lax.rem(row + d, R), col)) for d in range(1, R)
    ]
    for d, copy in enumerate(copies):
        copy.wait_recv()
        total = total + red2_in[d]
    total = jnp.sum(total, axis=1, keepdims=True)
    number = [total[n : n + 1, :] for n in range(sums)]

    matrix = [[None] * (ITERS + 1) for _ in range(ITERS)]
    for n, (j, k) in enumerate(pairs):
        matrix[j][k] = matrix[k][j] = number[n]
    for k in range(ITERS):
        matrix[k][ITERS] = number[len(pairs) + k]
    for i in range(ITERS):
        inverse = 1.0 / matrix[i][i]
        for k in range(i + 1, ITERS + 1):
            matrix[i][k] = matrix[i][k] * inverse
        for j in range(i + 1, ITERS):
            for k in range(i + 1, ITERS + 1):
                matrix[j][k] = matrix[j][k] - matrix[j][i] * matrix[i][k]
    coef = [None] * ITERS
    for i in reversed(range(ITERS)):
        coef[i] = matrix[i][ITERS]
        for k in range(i + 1, ITERS):
            coef[i] = coef[i] - matrix[i][k] * coef[k]

    def finish(i, carry):
        at = pl.ds(pl.multiple_of(i * step, step), step)
        inner = pl.ds(pl.multiple_of(16 + i * step, 8), step)
        value = coef[0] * V[0, inner, 0:TC]
        for k in range(1, ITERS):
            value = value + coef[k] * V[k, inner, 0:TC]
        x_out[at, :] = value
        high, low = halves(value)
        seen = dot(high.astype(BF16), B[...]) + dot(low.astype(BF16), B[...])
        place = lax.broadcasted_iota(jnp.int32, (step, S), 0) + i * step
        return carry + jnp.sum(jnp.where(place == fine_row, seen, 0.0), axis=0, keepdims=True)

    at_fine = lax.fori_loop(0, TR // step, finish, jnp.zeros((1, S), F32))
    for o in range(C):
        fval_out[o] = at_fine[:, o * per : (o + 1) * per]
    fval_in[col] = fval_out[col]
    copies = [
        send(fval_out.at[lax.rem(col + d, C)], fval_in.at[col], (row, lax.rem(col + d, C)))
        for d in range(1, C)
    ]

    place = lax.broadcasted_iota(jnp.int32, (BR, BC), 1)
    place_v = lax.broadcasted_iota(jnp.int32, (BR, BC), 0)
    within = remainder(place, GROUP)

    def beside(volt, n):
        above = jnp.where(place_v == 0, keep(top_ok, crow_top[n, 7:8, :]), pltpu.roll(volt, 1, 0))
        below = jnp.where(
            place_v == BR - 1, keep(bot_ok, crow_bot[n, 0:1, :]), pltpu.roll(volt, BR - 1, 0)
        )
        far_left, far_right = cleft[n], cright[n]
        turned_left = jnp.where(place == 0, 0.0, pltpu.roll(far_left, 1, 1))
        plain_left = pltpu.roll(far_left, BC - GROUP + 1, 1)
        from_left = jnp.where(left_ok, plain_left, turned_left)
        turned_right = jnp.where(place == BC - 1, 0.0, pltpu.roll(far_right, BC - 1, 1))
        plain_right = pltpu.roll(far_right, GROUP - 1, 1)
        from_right = jnp.where(right_ok, plain_right, turned_right)
        before = jnp.where(within == 0, from_left, pltpu.roll(volt, 1, 1))
        after = jnp.where(within == GROUP - 1, from_right, pltpu.roll(volt, BC - 1, 1))
        return above + below + before + after

    for copy in coarse0:
        copy.wait_recv()
    volt = cinit[...]
    scale = relaxation / coarse_diag
    partial = volt + scale * (coarse_conductance * beside(volt, 0) - coarse_diag * volt)
    for copy in copies:
        copy.wait_recv()
    amount = in_weight * jnp.concatenate([fval_in[t] for t in range(C)], axis=1)
    hi, lo = halves(amount)
    sources = onto_coarse(hi) + onto_coarse(lo)
    volt = partial + scale * sources
    volt1[...] = volt
    coarse1 = coarse_send(volt1, 1)
    partial = volt + scale * (sources - coarse_diag * volt)
    for copy in coarse1:
        copy.wait_recv()
    c_out[...] = partial + scale * (coarse_conductance * beside(volt, 1))
    for copy in pending:
        copy.wait_send()


def per_device(R, C, load_amp, load_mask, leak, coarse_leak, coarse_init, via_fine, via_coarse, via_count):
    TR, TC = leak.shape
    BR, BC = coarse_leak.shape
    S = via_fine.shape[1]
    per = S // C
    copies = 4 * (C - 1) + (R - 1) + 24
    vmem = pl.BlockSpec(memory_space=pltpu.VMEM)
    ext = (TR + 32, TC + LANES)
    return pl.pallas_call(
        functools.partial(kernel, R, C),
        out_shape=(jax.ShapeDtypeStruct((TR, TC), F32), jax.ShapeDtypeStruct((BR, BC), F32)),
        in_specs=[vmem] * 7 + [pl.BlockSpec(memory_space=pltpu.SMEM)],
        out_specs=(vmem, vmem),
        scratch_shapes=[
            pltpu.VMEM((C, 8, per), F32), pltpu.VMEM((C, 8, per), F32),
            pltpu.VMEM((C, 1, per), F32), pltpu.VMEM((C, 1, per), F32),
            pltpu.VMEM((C, 1, per), F32), pltpu.VMEM((C, 1, per), F32),
            pltpu.VMEM((TC, S), BF16),
            pltpu.VMEM((S, TC), BF16),
            pltpu.VMEM(ext, F32),
            pltpu.VMEM((ITERS,) + ext, F32),
            pltpu.VMEM((ITERS - 1,) + ext, F32),
            pltpu.VMEM((TR, TC), F32),
            pltpu.VMEM((2, TR, LANES), F32),
            pltpu.VMEM((2, LANES, TR), F32),
            pltpu.VMEM((2, LANES, TR), F32),
            pltpu.VMEM((2, 8, TC), F32),
            pltpu.VMEM((2, 8, TC), F32),
            pltpu.VMEM((2, 4, 8, LANES), F32),
            pltpu.VMEM((16, LANES), F32), pltpu.VMEM((C - 1, 16, LANES), F32),
            pltpu.VMEM((16, LANES), F32), pltpu.VMEM((R - 1, 16, LANES), F32),
            pltpu.VMEM((BR, BC), F32),
            pltpu.VMEM((2, 8, BC), F32), pltpu.VMEM((2, 8, BC), F32),
            pltpu.VMEM((2, BR, BC), F32), pltpu.VMEM((2, BR, BC), F32),
            pltpu.SemaphoreType.DMA((copies,)),
            pltpu.SemaphoreType.DMA((copies,)),
        ],
        compiler_params=pltpu.CompilerParams(
            collective_id=0, has_side_effects=True, vmem_limit_bytes=48 * 1024 * 1024
        ),
    )(load_amp, load_mask, leak, coarse_leak, coarse_init, via_fine, via_coarse, via_count)


def solution(mesh):
    spec = P("row", "col")
    return jax.shard_map(
        functools.partial(per_device, mesh.shape["row"], mesh.shape["col"]),
        mesh=mesh, in_specs=(spec,) * 8, out_specs=(spec, spec), check_vma=False,
    )
```

```python
import functools
import jax
import jax.numpy as jnp
from jax import lax
from jax.experimental import pallas as pl
from jax.experimental.pallas import tpu as pltpu
from jax.sharding import PartitionSpec as P

GROUP = 16
ITERS = 4
LANES = 128

via_conductance = 2.0
coarse_conductance = 4.0
relaxation = 0.8

F32 = jnp.float32
BF16 = jnp.bfloat16


def divide(value, by):
    if by & (by - 1) == 0:
        return lax.shift_right_logical(value, by.bit_length() - 1)
    return value // by


def remainder(value, by):
    if by & (by - 1) == 0:
        return value & (by - 1)
    return value % by


def halves(value):
    high = value.astype(BF16).astype(F32)
    return high, value - high


def dot(a, b):
    return jnp.dot(a, b, preferred_element_type=F32)


def chunk_of(rows, top):
    size = top
    while rows % size:
        size -= 8
    return size


def kernel(
    R, C,
    amp_in, mask_in, leak_in, cleak_in, cinit_in, vf_in, vc_in, cnt_in,
    x_out, c_out,
    amp, mask, leak, cleak, cinit, vf, vc, cnt, load_sem, xv,
    msg_out, msg_in, val_out, val_in, fval_out, fval_in,
    B, Bt, dv, V, Y, rhs,
    E, ET, H, rtop, rbot, rcorner,
    red_out, red_in, red2_out, red2_in,
    volt1, turn, seam_out, crow_top, crow_bot, cleft, cright,
    send_sem, recv_sem,
):
    row, col = lax.axis_index("row"), lax.axis_index("col")
    sources_of = (cnt_in, vc_in, vf_in, cinit_in, leak_in, cleak_in, amp_in, mask_in)
    targets_of = (cnt, vc, vf, cinit, leak, cleak, amp, mask)
    loads = [
        pltpu.make_async_copy(source, target, load_sem.at[n])
        for n, (source, target) in enumerate(zip(sources_of, targets_of))
    ]
    for load in loads:
        load.start()
    TR, TC = leak.shape
    BR, BC = cleak.shape
    S = vf.shape[1]
    per = S // C
    up, down = lax.rem(row + R - 1, R), lax.rem(row + 1, R)
    left, right = lax.rem(col + C - 1, C), lax.rem(col + 1, C)

    barrier = pltpu.get_barrier_semaphore()
    peers = [(row, lax.rem(col + d, C)) for d in range(1, C)]
    peers += [(lax.rem(row + d, R), col) for d in range(1, R)]
    peers += [(u, s) for u in (up, down) for s in (left, right)]
    for peer in peers:
        pl.semaphore_signal(barrier, inc=1, device_id=peer, device_id_type=pl.DeviceIdType.MESH)

    count = [0]
    pending = []

    def send(src, dst, device):
        n = count[0]
        count[0] += 1
        copy = pltpu.make_async_remote_copy(
            src_ref=src, dst_ref=dst, send_sem=send_sem.at[n], recv_sem=recv_sem.at[n],
            device_id=device, device_id_type=pl.DeviceIdType.MESH,
        )
        copy.start()
        pending.append(copy)
        return copy

    loads[0].wait()
    loads[1].wait()
    lane = lax.broadcasted_iota(jnp.int32, (1, per), 1)
    weight = jnp.concatenate(
        [jnp.where(lane < cnt[0, o], via_conductance, 0.0).astype(F32) for o in range(C)], axis=1
    )
    node = vc[...]
    node_row = divide(node, BC * C).astype(F32)
    node_col = remainder(node, BC).astype(F32)
    for o in range(C):
        cut = slice(o * per, (o + 1) * per)
        msg_out[o, 0:1, :] = node_row[:, cut]
        msg_out[o, 1:2, :] = node_col[:, cut]
        msg_out[o, 2:3, :] = weight[:, cut]
        msg_out[o, 3:8, :] = jnp.zeros((5, per), F32)
    msg_in[col] = msg_out[col]
    for n in range(2):
        H[n] = jnp.zeros((LANES, TR), F32)
    loads[2].wait()
    fine = vf[...]
    fine_row = divide(fine, TC)
    fine_col = remainder(fine, TC)
    step = 64

    def build_cols(i, carry):
        at = pl.ds(pl.multiple_of(i * step, step), step)
        place = lax.broadcasted_iota(jnp.int32, (step, S), 0) + i * step
        B[at, :] = jnp.where(place == fine_col, 1.0, 0.0).astype(BF16)
        return carry

    lax.fori_loop(0, TC // step, build_cols, 0)
    lanes = lax.broadcasted_iota(jnp.int32, (per, TC), 1).astype(F32)
    for o in range(C):
        cut = slice(o * per, (o + 1) * per)
        turned = jnp.broadcast_to(fine_col[:, cut].astype(F32), (LANES, per)).T
        wide = jnp.concatenate([turned] * (TC // LANES), axis=1)
        Bt[cut, :] = jnp.where(wide == lanes, 1.0, 0.0).astype(BF16)

    pl.semaphore_wait(barrier, len(peers))

    messages = [
        send(msg_out.at[lax.rem(col + d, C)], msg_in.at[col], (row, lax.rem(col + d, C)))
        for d in range(1, C)
    ]

    def coarse_send(ref, n):
        return [
            send(ref.at[pl.ds(0, 8)], crow_bot.at[n], (up, col)),
            send(ref.at[pl.ds(BR - 8, 8)], crow_top.at[n], (down, col)),
            send(seam_out.at[n, 0], cright.at[n], (row, left)),
            send(seam_out.at[n, 1], cleft.at[n], (row, right)),
        ]

    groups = BC // GROUP

    def seams(volt, n):
        turn[n] = volt.T
        seam_out[n, 0] = turn[n, pl.ds(0, groups, stride=GROUP), :]
        seam_out[n, 1] = turn[n, pl.ds(GROUP - 1, groups, stride=GROUP), :]

    loads[3].wait()
    seams(cinit[...], 0)
    coarse0 = coarse_send(cinit, 0)

    zero_pad = jnp.zeros((8, TC + LANES), F32)
    for n in range(ITERS):
        V[n, 0:8, :] = zero_pad
        V[n, TR + 24 : TR + 32, :] = zero_pad

    loads[4].wait()
    wide_step = 256 if TR % 256 == 0 else step
    half_step = wide_step // 2

    def diagonal(i, carry):
        at = pl.ds(pl.multiple_of(i * wide_step, wide_step), wide_step)
        inner = pl.ds(pl.multiple_of(16 + i * wide_step, 8), wide_step)
        place = lax.broadcasted_iota(jnp.int32, (wide_step, S), 0) + i * wide_step
        match = place == fine_row
        value = 4.0 + leak[at, :] + dot(jnp.where(match, weight, 0.0).astype(BF16), Bt[...])
        dv[inner, 0:TC] = 1.0 / value
        return carry

    lax.fori_loop(0, TR // wide_step, diagonal, 0)

    low_side = lax.broadcasted_iota(jnp.int32, (TR, LANES), 1) < LANES // 2

    def halo_send(F, n):
        edge = jnp.where(low_side, F[16 : 16 + TR, 0:LANES], F[16 : 16 + TR, TC - LANES : TC])
        E[n] = edge
        ET[n] = edge.T
        return [
            send(F.at[pl.ds(16, 8), pl.ds(0, TC)], rbot.at[n], (up, col)),
            send(F.at[pl.ds(TR + 8, 8), pl.ds(0, TC)], rtop.at[n], (down, col)),
            send(ET.at[n, pl.ds(0, 8)], H.at[n, pl.ds(0, 8)], (row, left)),
            send(ET.at[n, pl.ds(LANES - 8, 8)], H.at[n, pl.ds(LANES - 8, 8)], (row, right)),
            send(E.at[n, pl.ds(0, 8)], rcorner.at[n, 3], (up, left)),
            send(E.at[n, pl.ds(0, 8)], rcorner.at[n, 2], (up, right)),
            send(E.at[n, pl.ds(TR - 8, 8)], rcorner.at[n, 1], (down, left)),
            send(E.at[n, pl.ds(TR - 8, 8)], rcorner.at[n, 0], (down, right)),
        ]

    top_ok, bot_ok = row > 0, row < R - 1
    left_ok, right_ok = col > 0, col < C - 1

    def keep(ok, value):
        return value * jnp.where(ok, 1.0, 0.0).astype(F32)

    def halo_land(F, n, copies):
        for copy in copies:
            copy.wait_recv()
        F[8:16, 0:TC] = keep(top_ok, rtop[n])
        F[TR + 16 : TR + 24, 0:TC] = keep(bot_ok, rbot[n])
        side = H[n].T
        F[16 : 16 + TR, TC : TC + LANES] = jnp.where(
            low_side, keep(right_ok, side), keep(left_ok, side)
        )
        low8 = lax.broadcasted_iota(jnp.int32, (8, LANES), 1)
        near_low, near_high = low8 < 8, low8 >= LANES - 8

        def corner(ok, lo, hi):
            return keep(
                ok,
                jnp.where(near_low, keep(right_ok, lo), 0.0)
                + jnp.where(near_high, keep(left_ok, hi), 0.0),
            )

        F[8:16, TC : TC + LANES] = corner(top_ok, rcorner[n, 1], rcorner[n, 0])
        F[TR + 16 : TR + 24, TC : TC + LANES] = corner(bot_ok, rcorner[n, 3], rcorner[n, 2])

    for copy in messages:
        copy.wait_recv()
    heard = [msg_in[t] for t in range(C)]
    in_row = jnp.concatenate([m[0:1] for m in heard], axis=1).astype(jnp.int32)
    in_col = jnp.concatenate([m[1:2] for m in heard], axis=1).astype(jnp.int32)
    in_weight = jnp.concatenate([m[2:3] for m in heard], axis=1)
    place_r = lax.broadcasted_iota(jnp.int32, (BR, S), 0)
    place_c = lax.broadcasted_iota(jnp.int32, (BC, S), 0)
    row_hit = place_r == in_row
    col_hot = jnp.where(place_c == in_col, 1.0, 0.0).astype(BF16)
    hi, lo = halves(cinit[...])
    seen = dot(hi.astype(BF16), col_hot) + dot(lo.astype(BF16), col_hot)
    at_via = jnp.sum(jnp.where(row_hit, seen, 0.0), axis=0, keepdims=True)
    for t in range(C):
        val_out[t] = at_via[:, t * per : (t + 1) * per]
    val_in[col] = val_out[col]
    values = [
        send(val_out.at[lax.rem(col + d, C)], val_in.at[col], (row, lax.rem(col + d, C)))
        for d in range(1, C)
    ]

    dinv_copies = halo_send(dv, 0)

    def onto_coarse(amount):
        spread = jnp.where(row_hit, amount, 0.0).astype(BF16)
        return lax.dot_general(spread, col_hot, (((1,), (1,)), ((), ())), preferred_element_type=F32)

    loads[5].wait()
    coarse_diag = 4.0 * coarse_conductance + cleak[...] + onto_coarse(in_weight)

    for copy in values:
        copy.wait_recv()
    loads[6].wait()
    loads[7].wait()
    drops = weight * jnp.concatenate([val_in[o] for o in range(C)], axis=1)
    drop_hi, drop_lo = halves(drops)

    def inject(i, carry):
        at = pl.ds(pl.multiple_of(i * half_step, half_step), half_step)
        inner = pl.ds(pl.multiple_of(16 + i * half_step, 8), half_step)
        place = lax.broadcasted_iota(jnp.int32, (half_step, S), 0) + i * half_step
        match = place == fine_row
        both = [jnp.where(match, part, 0.0).astype(BF16) for part in (drop_hi, drop_lo)]
        both = dot(jnp.concatenate(both, axis=0), Bt[...])
        added = both[:half_step] + both[half_step:]
        value = amp[at, :] * mask[at, :].astype(F32) + added
        rhs[at, :] = value
        V[0, inner, 0:TC] = value * dv[inner, 0:TC]
        return carry

    lax.fori_loop(0, TR // half_step, inject, 0)
    first_copies = halo_send(V.at[0], 1)
    halo_land(dv, 0, dinv_copies)
    halo_land(V.at[0], 1, first_copies)

    rows = chunk_of(TR + 16, 48)
    width = TC + LANES

    def around(k, start, size):
        tall = V.at[k, pl.ds(pl.multiple_of(start - 8, 8), size + 16), :]
        mid = tall[8 : 8 + size, :]
        total = tall[7 : 7 + size, :] + tall[9 : 9 + size, :]
        return total + pltpu.roll(mid, 1, 1) + pltpu.roll(mid, width - 1, 1)

    for k in range(ITERS - 1):

        def advance(i, carry, k=k):
            start = pl.multiple_of(8 + i * rows, 8)
            near = around(k, start, rows)
            Y[k, pl.ds(start, rows), :] = near
            fresh = dv[pl.ds(start, rows), :] * near
            if k:
                fresh = 2.0 * fresh - V[k - 1, pl.ds(start, rows), :]
            V[k + 1, pl.ds(start, rows), :] = fresh
            return carry

        lax.fori_loop(0, (TR + 16) // rows, advance, 0)

    orders = 2 * ITERS - 1
    sums = orders + ITERS

    def fold(value):
        total = value[:, 0:LANES]
        for n in range(1, TC // LANES):
            total = total + value[:, n * LANES : (n + 1) * LANES]
        return total

    def gram(i, carry):
        at = pl.ds(pl.multiple_of(i * 8, 8), 8)
        start = pl.multiple_of(16 + i * 8, 8)
        inner = pl.ds(start, 8)
        v = [V[k, inner, 0:TC] for k in range(ITERS)]
        y = [Y[k, inner, 0:TC] for k in range(ITERS - 1)]
        y.append(around(ITERS - 1, start, 8)[:, 0:TC])
        w = [rhs[at, :], y[0]]
        for k in range(2, ITERS):
            w.append(2.0 * y[k - 1] - w[k - 2])
        applied = [w[k] - y[k] for k in range(ITERS)]
        fresh = [fold(v[0] * applied[k]) for k in range(ITERS)]
        fresh += [fold(v[ITERS - 1] * applied[k]) for k in range(1, ITERS)]
        fresh += [fold(w[0] * v[k]) for k in range(ITERS)]
        return tuple(a + b for a, b in zip(carry, fresh))

    totals = lax.fori_loop(0, TR // 8, gram, tuple(jnp.zeros((8, LANES), F32) for _ in range(sums)))
    red_out[...] = jnp.zeros(red_out.shape, F32)
    for n, total in enumerate(totals):
        red_out[n : n + 1, :] = jnp.sum(total, axis=0, keepdims=True)
    copies = [
        send(red_out, red_in.at[d - 1], (row, lax.rem(col + d, C))) for d in range(1, C)
    ]
    total = red_out[...]
    for d, copy in enumerate(copies):
        copy.wait_recv()
        total = total + red_in[d]
    red2_out[...] = total
    copies = [
        send(red2_out, red2_in.at[d - 1], (lax.rem(row + d, R), col)) for d in range(1, R)
    ]
    for d, copy in enumerate(copies):
        copy.wait_recv()
        total = total + red2_in[d]
    total = jnp.sum(total, axis=1, keepdims=True)
    number = [total[n : n + 1, :] for n in range(sums)]

    matrix = [[None] * (ITERS + 1) for _ in range(ITERS)]
    for n in range(ITERS, orders):
        number[n] = 2.0 * number[n] - number[2 * (ITERS - 1) - n]
    for j in range(ITERS):
        for k in range(j + 1):
            matrix[j][k] = matrix[k][j] = 0.5 * (number[j + k] + number[j - k])
        matrix[j][ITERS] = number[orders + j]
    for i in range(ITERS):
        inverse = 1.0 / matrix[i][i]
        for k in range(i + 1, ITERS + 1):
            matrix[i][k] = matrix[i][k] * inverse
        for j in range(i + 1, ITERS):
            for k in range(i + 1, ITERS + 1):
                matrix[j][k] = matrix[j][k] - matrix[j][i] * matrix[i][k]
    coef = [None] * ITERS
    for i in reversed(range(ITERS)):
        coef[i] = matrix[i][ITERS]
        for k in range(i + 1, ITERS):
            coef[i] = coef[i] - matrix[i][k] * coef[k]

    def finish(i, carry):
        at = pl.ds(pl.multiple_of(i * half_step, half_step), half_step)
        inner = pl.ds(pl.multiple_of(16 + i * half_step, 8), half_step)
        value = coef[0] * V[0, inner, 0:TC]
        for k in range(1, ITERS):
            value = value + coef[k] * V[k, inner, 0:TC]
        xv[at, :] = value
        high, low = halves(value)
        both = dot(jnp.concatenate([high.astype(BF16), low.astype(BF16)], axis=0), B[...])
        seen = both[:half_step] + both[half_step:]
        place = lax.broadcasted_iota(jnp.int32, (half_step, S), 0) + i * half_step
        return carry + jnp.sum(jnp.where(place == fine_row, seen, 0.0), axis=0, keepdims=True)

    at_fine = lax.fori_loop(0, TR // half_step, finish, jnp.zeros((1, S), F32))
    store = pltpu.make_async_copy(xv, x_out, load_sem.at[8])
    for o in range(C):
        fval_out[o] = at_fine[:, o * per : (o + 1) * per]
    fval_in[col] = fval_out[col]
    copies = [
        send(fval_out.at[lax.rem(col + d, C)], fval_in.at[col], (row, lax.rem(col + d, C)))
        for d in range(1, C)
    ]

    store.start()
    place = lax.broadcasted_iota(jnp.int32, (BR, BC), 1)
    place_v = lax.broadcasted_iota(jnp.int32, (BR, BC), 0)
    within = remainder(place, GROUP)

    def beside(volt, n):
        above = jnp.where(place_v == 0, keep(top_ok, crow_top[n, 7:8, :]), pltpu.roll(volt, 1, 0))
        below = jnp.where(
            place_v == BR - 1, keep(bot_ok, crow_bot[n, 0:1, :]), pltpu.roll(volt, BR - 1, 0)
        )
        group = lax.broadcasted_iota(jnp.int32, (groups, BR), 0)
        far = cleft[n]
        turn[n, pl.ds(0, groups, stride=GROUP), :] = jnp.where(
            left_ok, far, jnp.where(group == 0, 0.0, jnp.roll(far, 1, 0))
        )
        far = cright[n]
        turn[n, pl.ds(GROUP - 1, groups, stride=GROUP), :] = jnp.where(
            right_ok, far, jnp.where(group == groups - 1, 0.0, jnp.roll(far, -1, 0))
        )
        edge = turn[n].T
        before = jnp.where(within == 0, edge, pltpu.roll(volt, 1, 1))
        after = jnp.where(within == GROUP - 1, edge, pltpu.roll(volt, BC - 1, 1))
        return above + below + before + after

    for copy in coarse0:
        copy.wait_recv()
    volt = cinit[...]
    scale = relaxation / coarse_diag
    partial = volt + scale * (coarse_conductance * beside(volt, 0) - coarse_diag * volt)
    for copy in copies:
        copy.wait_recv()
    amount = in_weight * jnp.concatenate([fval_in[t] for t in range(C)], axis=1)
    hi, lo = halves(amount)
    sources = onto_coarse(hi) + onto_coarse(lo)
    volt = partial + scale * sources
    volt1[...] = volt
    seams(volt, 1)
    coarse1 = coarse_send(volt1, 1)
    partial = volt + scale * (sources - coarse_diag * volt)
    for copy in coarse1:
        copy.wait_recv()
    c_out[...] = partial + scale * (coarse_conductance * beside(volt, 1))
    store.wait()
    for copy in pending:
        copy.wait_send()


def per_device(R, C, load_amp, load_mask, leak, coarse_leak, coarse_init, via_fine, via_coarse, via_count):
    TR, TC = leak.shape
    BR, BC = coarse_leak.shape
    S = via_fine.shape[1]
    per = S // C
    copies = 4 * (C - 1) + (R - 1) + 24
    vmem = pl.BlockSpec(memory_space=pltpu.VMEM)
    ext = (TR + 32, TC + LANES)
    return pl.pallas_call(
        functools.partial(kernel, R, C),
        out_shape=(jax.ShapeDtypeStruct((TR, TC), F32), jax.ShapeDtypeStruct((BR, BC), F32)),
        in_specs=[pl.BlockSpec(memory_space=pltpu.HBM)] * 8,
        out_specs=(pl.BlockSpec(memory_space=pltpu.HBM), vmem),
        scratch_shapes=[
            pltpu.VMEM((TR, TC), F32), pltpu.VMEM((TR, TC), jnp.int32), pltpu.VMEM((TR, TC), F32),
            pltpu.VMEM((BR, BC), F32), pltpu.VMEM((BR, BC), F32),
            pltpu.VMEM((1, S), jnp.int32), pltpu.VMEM((1, S), jnp.int32),
            pltpu.SMEM((1, C), jnp.int32), pltpu.SemaphoreType.DMA((9,)), pltpu.VMEM((TR, TC), F32),
            pltpu.VMEM((C, 8, per), F32), pltpu.VMEM((C, 8, per), F32),
            pltpu.VMEM((C, 1, per), F32), pltpu.VMEM((C, 1, per), F32),
            pltpu.VMEM((C, 1, per), F32), pltpu.VMEM((C, 1, per), F32),
            pltpu.VMEM((TC, S), BF16),
            pltpu.VMEM((S, TC), BF16),
            pltpu.VMEM(ext, F32),
            pltpu.VMEM((ITERS,) + ext, F32),
            pltpu.VMEM((ITERS - 1,) + ext, F32),
            pltpu.VMEM((TR, TC), F32),
            pltpu.VMEM((2, TR, LANES), F32),
            pltpu.VMEM((2, LANES, TR), F32),
            pltpu.VMEM((2, LANES, TR), F32),
            pltpu.VMEM((2, 8, TC), F32),
            pltpu.VMEM((2, 8, TC), F32),
            pltpu.VMEM((2, 4, 8, LANES), F32),
            pltpu.VMEM((16, LANES), F32), pltpu.VMEM((C - 1, 16, LANES), F32),
            pltpu.VMEM((16, LANES), F32), pltpu.VMEM((R - 1, 16, LANES), F32),
            pltpu.VMEM((BR, BC), F32),
            pltpu.VMEM((2, BC, BR), F32), pltpu.VMEM((2, 2, BC // GROUP, BR), F32),
            pltpu.VMEM((2, 8, BC), F32), pltpu.VMEM((2, 8, BC), F32),
            pltpu.VMEM((2, BC // GROUP, BR), F32), pltpu.VMEM((2, BC // GROUP, BR), F32),
            pltpu.SemaphoreType.DMA((copies,)),
            pltpu.SemaphoreType.DMA((copies,)),
        ],
        compiler_params=pltpu.CompilerParams(
            collective_id=0, has_side_effects=True, vmem_limit_bytes=60 * 1024 * 1024
        ),
    )(load_amp, load_mask, leak, coarse_leak, coarse_init, via_fine, via_coarse, via_count)


def solution(mesh):
    spec = P("row", "col")
    return jax.shard_map(
        functools.partial(per_device, mesh.shape["row"], mesh.shape["col"]),
        mesh=mesh, in_specs=(spec,) * 8, out_specs=(spec, spec), check_vma=False,
    )
```

```python
import functools
import jax
import jax.numpy as jnp
from jax import lax
from jax.experimental import pallas as pl
from jax.experimental.pallas import tpu as pltpu
from jax.sharding import PartitionSpec as P

GROUP = 16
ITERS = 4
LANES = 128

via_conductance = 2.0
coarse_conductance = 4.0
relaxation = 0.8

F32 = jnp.float32
BF16 = jnp.bfloat16


def divide(value, by):
    if by & (by - 1) == 0:
        return lax.shift_right_logical(value, by.bit_length() - 1)
    return value // by


def remainder(value, by):
    if by & (by - 1) == 0:
        return value & (by - 1)
    return value % by


def halves(value):
    high = value.astype(BF16).astype(F32)
    return high, value - high


def dot(a, b):
    return jnp.dot(a, b, preferred_element_type=F32)


def chunk_of(rows, top):
    size = top
    while rows % size:
        size -= 8
    return size


def kernel(
    R, C,
    amp_in, mask_in, leak_in, cleak_in, cinit_in, vf_in, vc_in, cnt_in,
    x_out, c_out,
    amp, mask, leak, cleak, cinit, vf, vc, cnt, load_sem, xv,
    msg_out, msg_in, val_out, val_in, fval_out, fval_in,
    B, Bt, dv, V, Y, rhs,
    E, ET, H, rtop, rbot, rcorner,
    red_out, red_in, red2_out, red2_in,
    volt1, turn, seam_out, crow_top, crow_bot, cleft, cright,
    send_sem, recv_sem,
):
    row, col = lax.axis_index("row"), lax.axis_index("col")
    sources_of = (cnt_in, vc_in, vf_in, cinit_in, leak_in, cleak_in, amp_in, mask_in)
    targets_of = (cnt, vc, vf, cinit, leak, cleak, amp, mask)
    loads = [
        pltpu.make_async_copy(source, target, load_sem.at[n])
        for n, (source, target) in enumerate(zip(sources_of, targets_of))
    ]
    for load in loads:
        load.start()
    TR, TC = leak.shape
    BR, BC = cleak.shape
    S = vf.shape[1]
    per = S // C
    up, down = lax.rem(row + R - 1, R), lax.rem(row + 1, R)
    left, right = lax.rem(col + C - 1, C), lax.rem(col + 1, C)

    barrier = pltpu.get_barrier_semaphore()
    peers = [(row, lax.rem(col + d, C)) for d in range(1, C)]
    peers += [(lax.rem(row + d, R), col) for d in range(1, R)]
    peers += [(u, s) for u in (up, down) for s in (left, right)]
    for peer in peers:
        pl.semaphore_signal(barrier, inc=1, device_id=peer, device_id_type=pl.DeviceIdType.MESH)

    count = [0]
    pending = []

    def send(src, dst, device):
        n = count[0]
        count[0] += 1
        copy = pltpu.make_async_remote_copy(
            src_ref=src, dst_ref=dst, send_sem=send_sem.at[n], recv_sem=recv_sem.at[n],
            device_id=device, device_id_type=pl.DeviceIdType.MESH,
        )
        copy.start()
        pending.append(copy)
        return copy

    loads[0].wait()
    loads[1].wait()
    lane = lax.broadcasted_iota(jnp.int32, (1, per), 1)
    weight = jnp.concatenate(
        [jnp.where(lane < cnt[0, o], via_conductance, 0.0).astype(F32) for o in range(C)], axis=1
    )
    node = vc[...]
    node_row = divide(node, BC * C).astype(F32)
    node_col = remainder(node, BC).astype(F32)
    for o in range(C):
        cut = slice(o * per, (o + 1) * per)
        msg_out[o, 0:1, :] = node_row[:, cut]
        msg_out[o, 1:2, :] = node_col[:, cut]
        msg_out[o, 2:3, :] = weight[:, cut]
        msg_out[o, 3:8, :] = jnp.zeros((5, per), F32)
    msg_in[col] = msg_out[col]
    for n in range(2):
        H[n] = jnp.zeros((LANES, TR), F32)
    loads[2].wait()
    fine = vf[...]
    fine_row = divide(fine, TC)
    fine_col = remainder(fine, TC)
    step = 64

    def build_cols(i, carry):
        at = pl.ds(pl.multiple_of(i * step, step), step)
        place = lax.broadcasted_iota(jnp.int32, (step, S), 0) + i * step
        B[at, :] = jnp.where(place == fine_col, 1.0, 0.0).astype(BF16)
        return carry

    lax.fori_loop(0, TC // step, build_cols, 0)
    lanes = lax.broadcasted_iota(jnp.int32, (per, TC), 1).astype(F32)
    for o in range(C):
        cut = slice(o * per, (o + 1) * per)
        turned = jnp.broadcast_to(fine_col[:, cut].astype(F32), (LANES, per)).T
        wide = jnp.concatenate([turned] * (TC // LANES), axis=1)
        Bt[cut, :] = jnp.where(wide == lanes, 1.0, 0.0).astype(BF16)

    pl.semaphore_wait(barrier, len(peers))

    messages = [
        send(msg_out.at[lax.rem(col + d, C)], msg_in.at[col], (row, lax.rem(col + d, C)))
        for d in range(1, C)
    ]

    def coarse_send(ref, n):
        return [
            send(ref.at[pl.ds(0, 8)], crow_bot.at[n], (up, col)),
            send(ref.at[pl.ds(BR - 8, 8)], crow_top.at[n], (down, col)),
            send(seam_out.at[n, 0], cright.at[n], (row, left)),
            send(seam_out.at[n, 1], cleft.at[n], (row, right)),
        ]

    groups = BC // GROUP

    def seams(volt, n):
        turn[n] = volt.T
        seam_out[n, 0] = turn[n, pl.ds(0, groups, stride=GROUP), :]
        seam_out[n, 1] = turn[n, pl.ds(GROUP - 1, groups, stride=GROUP), :]

    loads[3].wait()
    seams(cinit[...], 0)
    coarse0 = coarse_send(cinit, 0)

    zero_pad = jnp.zeros((8, TC + LANES), F32)
    for n in range(ITERS):
        V[n, 0:8, :] = zero_pad
        V[n, TR + 24 : TR + 32, :] = zero_pad

    loads[4].wait()
    wide_step = 256 if TR % 256 == 0 else step
    half_step = wide_step // 2

    def diagonal(i, carry):
        at = pl.ds(pl.multiple_of(i * wide_step, wide_step), wide_step)
        inner = pl.ds(pl.multiple_of(16 + i * wide_step, 8), wide_step)
        place = lax.broadcasted_iota(jnp.int32, (wide_step, S), 0) + i * wide_step
        match = place == fine_row
        value = 4.0 + leak[at, :] + dot(jnp.where(match, weight, 0.0).astype(BF16), Bt[...])
        dv[inner, 0:TC] = 1.0 / value
        return carry

    lax.fori_loop(0, TR // wide_step, diagonal, 0)

    low_side = lax.broadcasted_iota(jnp.int32, (TR, LANES), 1) < LANES // 2

    def halo_send(F, n):
        edge = jnp.where(low_side, F[16 : 16 + TR, 0:LANES], F[16 : 16 + TR, TC - LANES : TC])
        E[n] = edge
        ET[n] = edge.T
        return [
            send(F.at[pl.ds(16, 8), pl.ds(0, TC)], rbot.at[n], (up, col)),
            send(F.at[pl.ds(TR + 8, 8), pl.ds(0, TC)], rtop.at[n], (down, col)),
            send(ET.at[n, pl.ds(0, 8)], H.at[n, pl.ds(0, 8)], (row, left)),
            send(ET.at[n, pl.ds(LANES - 8, 8)], H.at[n, pl.ds(LANES - 8, 8)], (row, right)),
            send(E.at[n, pl.ds(0, 8)], rcorner.at[n, 3], (up, left)),
            send(E.at[n, pl.ds(0, 8)], rcorner.at[n, 2], (up, right)),
            send(E.at[n, pl.ds(TR - 8, 8)], rcorner.at[n, 1], (down, left)),
            send(E.at[n, pl.ds(TR - 8, 8)], rcorner.at[n, 0], (down, right)),
        ]

    top_ok, bot_ok = row > 0, row < R - 1
    left_ok, right_ok = col > 0, col < C - 1

    def keep(ok, value):
        return value * jnp.where(ok, 1.0, 0.0).astype(F32)

    def halo_land(F, n, copies):
        for copy in copies:
            copy.wait_recv()
        F[8:16, 0:TC] = keep(top_ok, rtop[n])
        F[TR + 16 : TR + 24, 0:TC] = keep(bot_ok, rbot[n])
        side = H[n].T
        F[16 : 16 + TR, TC : TC + LANES] = jnp.where(
            low_side, keep(right_ok, side), keep(left_ok, side)
        )
        low8 = lax.broadcasted_iota(jnp.int32, (8, LANES), 1)
        near_low, near_high = low8 < 8, low8 >= LANES - 8

        def corner(ok, lo, hi):
            return keep(
                ok,
                jnp.where(near_low, keep(right_ok, lo), 0.0)
                + jnp.where(near_high, keep(left_ok, hi), 0.0),
            )

        F[8:16, TC : TC + LANES] = corner(top_ok, rcorner[n, 1], rcorner[n, 0])
        F[TR + 16 : TR + 24, TC : TC + LANES] = corner(bot_ok, rcorner[n, 3], rcorner[n, 2])

    for copy in messages:
        copy.wait_recv()
    heard = [msg_in[t] for t in range(C)]
    in_row = jnp.concatenate([m[0:1] for m in heard], axis=1).astype(jnp.int32)
    in_col = jnp.concatenate([m[1:2] for m in heard], axis=1).astype(jnp.int32)
    in_weight = jnp.concatenate([m[2:3] for m in heard], axis=1)
    place_r = lax.broadcasted_iota(jnp.int32, (BR, S), 0)
    place_c = lax.broadcasted_iota(jnp.int32, (BC, S), 0)
    row_hit = place_r == in_row
    col_hot = jnp.where(place_c == in_col, 1.0, 0.0).astype(BF16)
    hi, lo = halves(cinit[...])
    seen = dot(hi.astype(BF16), col_hot) + dot(lo.astype(BF16), col_hot)
    at_via = jnp.sum(jnp.where(row_hit, seen, 0.0), axis=0, keepdims=True)
    for t in range(C):
        val_out[t] = at_via[:, t * per : (t + 1) * per]
    val_in[col] = val_out[col]
    values = [
        send(val_out.at[lax.rem(col + d, C)], val_in.at[col], (row, lax.rem(col + d, C)))
        for d in range(1, C)
    ]

    dinv_copies = halo_send(dv, 0)

    def onto_coarse(amount):
        spread = jnp.where(row_hit, amount, 0.0).astype(BF16)
        return lax.dot_general(spread, col_hot, (((1,), (1,)), ((), ())), preferred_element_type=F32)

    loads[5].wait()
    coarse_diag = 4.0 * coarse_conductance + cleak[...] + onto_coarse(in_weight)

    for copy in values:
        copy.wait_recv()
    loads[6].wait()
    loads[7].wait()
    drops = weight * jnp.concatenate([val_in[o] for o in range(C)], axis=1)
    drop_hi, drop_lo = halves(drops)

    def inject(i, carry):
        at = pl.ds(pl.multiple_of(i * half_step, half_step), half_step)
        inner = pl.ds(pl.multiple_of(16 + i * half_step, 8), half_step)
        place = lax.broadcasted_iota(jnp.int32, (half_step, S), 0) + i * half_step
        match = place == fine_row
        both = [jnp.where(match, part, 0.0).astype(BF16) for part in (drop_hi, drop_lo)]
        both = dot(jnp.concatenate(both, axis=0), Bt[...])
        added = both[:half_step] + both[half_step:]
        value = amp[at, :] * mask[at, :].astype(F32) + added
        rhs[at, :] = value
        V[0, inner, 0:TC] = value * dv[inner, 0:TC]
        return carry

    lax.fori_loop(0, TR // half_step, inject, 0)
    first_copies = halo_send(V.at[0], 1)
    halo_land(dv, 0, dinv_copies)
    halo_land(V.at[0], 1, first_copies)

    rows = chunk_of(TR + 16, 48)
    width = TC + LANES

    def around(k, start, size):
        tall = V[k, pl.ds(pl.multiple_of(start - 8, 8), size + 16), :]
        mid = tall[8 : 8 + size]
        total = pltpu.roll(tall, 1, 0)[8 : 8 + size] + pltpu.roll(tall, size + 15, 0)[8 : 8 + size]
        return total + pltpu.roll(mid, 1, 1) + pltpu.roll(mid, width - 1, 1)

    for k in range(ITERS - 1):

        def advance(i, carry, k=k):
            start = pl.multiple_of(8 + i * rows, 8)
            near = around(k, start, rows)
            Y[k, pl.ds(start, rows), :] = near
            fresh = dv[pl.ds(start, rows), :] * near
            if k:
                fresh = 2.0 * fresh - V[k - 1, pl.ds(start, rows), :]
            V[k + 1, pl.ds(start, rows), :] = fresh
            return carry

        lax.fori_loop(0, (TR + 16) // rows, advance, 0)

    orders = 2 * ITERS - 1
    sums = orders + ITERS

    def fold(value):
        total = value[:, 0:LANES]
        for n in range(1, TC // LANES):
            total = total + value[:, n * LANES : (n + 1) * LANES]
        return total

    def gram(i, carry):
        at = pl.ds(pl.multiple_of(i * 8, 8), 8)
        start = pl.multiple_of(16 + i * 8, 8)
        inner = pl.ds(start, 8)
        v = [V[k, inner, 0:TC] for k in range(ITERS)]
        y = [Y[k, inner, 0:TC] for k in range(ITERS - 1)]
        y.append(around(ITERS - 1, start, 8)[:, 0:TC])
        w = [rhs[at, :], y[0]]
        for k in range(2, ITERS):
            w.append(2.0 * y[k - 1] - w[k - 2])
        applied = [w[k] - y[k] for k in range(ITERS)]
        fresh = [fold(v[0] * applied[k]) for k in range(ITERS)]
        fresh += [fold(v[ITERS - 1] * applied[k]) for k in range(1, ITERS)]
        fresh += [fold(w[0] * v[k]) for k in range(ITERS)]
        return tuple(a + b for a, b in zip(carry, fresh))

    totals = lax.fori_loop(0, TR // 8, gram, tuple(jnp.zeros((8, LANES), F32) for _ in range(sums)))
    red_out[...] = jnp.zeros(red_out.shape, F32)
    for n, total in enumerate(totals):
        red_out[n : n + 1, :] = jnp.sum(total, axis=0, keepdims=True)
    copies = [
        send(red_out, red_in.at[d - 1], (row, lax.rem(col + d, C))) for d in range(1, C)
    ]

    def gather(k):
        def body(i, carry):
            inner = pl.ds(pl.multiple_of(16 + i * half_step, 8), half_step)
            high, low = halves(V[k, inner, 0:TC])
            both = dot(jnp.concatenate([high.astype(BF16), low.astype(BF16)], axis=0), B[...])
            seen = both[:half_step] + both[half_step:]
            place = lax.broadcasted_iota(jnp.int32, (half_step, S), 0) + i * half_step
            return carry + jnp.sum(jnp.where(place == fine_row, seen, 0.0), axis=0, keepdims=True)

        return lax.fori_loop(0, TR // half_step, body, jnp.zeros((1, S), F32))

    seen_at = [gather(k) for k in range(ITERS // 2)]
    total = red_out[...]
    for d, copy in enumerate(copies):
        copy.wait_recv()
        total = total + red_in[d]
    red2_out[...] = total
    copies = [
        send(red2_out, red2_in.at[d - 1], (lax.rem(row + d, R), col)) for d in range(1, R)
    ]
    seen_at += [gather(k) for k in range(ITERS // 2, ITERS)]
    for d, copy in enumerate(copies):
        copy.wait_recv()
        total = total + red2_in[d]
    total = jnp.sum(total, axis=1, keepdims=True)
    number = [total[n : n + 1, :] for n in range(sums)]

    matrix = [[None] * (ITERS + 1) for _ in range(ITERS)]
    for n in range(ITERS, orders):
        number[n] = 2.0 * number[n] - number[2 * (ITERS - 1) - n]
    for j in range(ITERS):
        for k in range(j + 1):
            matrix[j][k] = matrix[k][j] = 0.5 * (number[j + k] + number[j - k])
        matrix[j][ITERS] = number[orders + j]
    for i in range(ITERS):
        inverse = 1.0 / matrix[i][i]
        for k in range(i + 1, ITERS + 1):
            matrix[i][k] = matrix[i][k] * inverse
        for j in range(i + 1, ITERS):
            for k in range(i + 1, ITERS + 1):
                matrix[j][k] = matrix[j][k] - matrix[j][i] * matrix[i][k]
    coef = [None] * ITERS
    for i in reversed(range(ITERS)):
        coef[i] = matrix[i][ITERS]
        for k in range(i + 1, ITERS):
            coef[i] = coef[i] - matrix[i][k] * coef[k]

    at_fine = coef[0] * seen_at[0]
    for k in range(1, ITERS):
        at_fine = at_fine + coef[k] * seen_at[k]
    store = pltpu.make_async_copy(xv, x_out, load_sem.at[8])
    for o in range(C):
        fval_out[o] = at_fine[:, o * per : (o + 1) * per]
    fval_in[col] = fval_out[col]
    copies = [
        send(fval_out.at[lax.rem(col + d, C)], fval_in.at[col], (row, lax.rem(col + d, C)))
        for d in range(1, C)
    ]


    def finish(i, carry):
        at = pl.ds(pl.multiple_of(i * step, step), step)
        inner = pl.ds(pl.multiple_of(16 + i * step, 8), step)
        value = coef[0] * V[0, inner, 0:TC]
        for k in range(1, ITERS):
            value = value + coef[k] * V[k, inner, 0:TC]
        xv[at, :] = value
        return carry

    lax.fori_loop(0, TR // step, finish, 0)
    store.start()
    place = lax.broadcasted_iota(jnp.int32, (BR, BC), 1)
    place_v = lax.broadcasted_iota(jnp.int32, (BR, BC), 0)
    within = remainder(place, GROUP)

    def beside(volt, n):
        above = jnp.where(place_v == 0, keep(top_ok, crow_top[n, 7:8, :]), pltpu.roll(volt, 1, 0))
        below = jnp.where(
            place_v == BR - 1, keep(bot_ok, crow_bot[n, 0:1, :]), pltpu.roll(volt, BR - 1, 0)
        )
        group = lax.broadcasted_iota(jnp.int32, (groups, BR), 0)
        far = cleft[n]
        turn[n, pl.ds(0, groups, stride=GROUP), :] = jnp.where(
            left_ok, far, jnp.where(group == 0, 0.0, jnp.roll(far, 1, 0))
        )
        far = cright[n]
        turn[n, pl.ds(GROUP - 1, groups, stride=GROUP), :] = jnp.where(
            right_ok, far, jnp.where(group == groups - 1, 0.0, jnp.roll(far, -1, 0))
        )
        edge = turn[n].T
        before = jnp.where(within == 0, edge, pltpu.roll(volt, 1, 1))
        after = jnp.where(within == GROUP - 1, edge, pltpu.roll(volt, BC - 1, 1))
        return above + below + before + after

    for copy in coarse0:
        copy.wait_recv()
    volt = cinit[...]
    scale = relaxation / coarse_diag
    partial = volt + scale * (coarse_conductance * beside(volt, 0) - coarse_diag * volt)
    for copy in copies:
        copy.wait_recv()
    amount = in_weight * jnp.concatenate([fval_in[t] for t in range(C)], axis=1)
    hi, lo = halves(amount)
    sources = onto_coarse(hi) + onto_coarse(lo)
    volt = partial + scale * sources
    volt1[...] = volt
    seams(volt, 1)
    coarse1 = coarse_send(volt1, 1)
    partial = volt + scale * (sources - coarse_diag * volt)
    for copy in coarse1:
        copy.wait_recv()
    c_out[...] = partial + scale * (coarse_conductance * beside(volt, 1))
    store.wait()
    for copy in pending:
        copy.wait_send()


def per_device(R, C, load_amp, load_mask, leak, coarse_leak, coarse_init, via_fine, via_coarse, via_count):
    TR, TC = leak.shape
    BR, BC = coarse_leak.shape
    S = via_fine.shape[1]
    per = S // C
    copies = 4 * (C - 1) + (R - 1) + 24
    vmem = pl.BlockSpec(memory_space=pltpu.VMEM)
    ext = (TR + 32, TC + LANES)
    return pl.pallas_call(
        functools.partial(kernel, R, C),
        out_shape=(jax.ShapeDtypeStruct((TR, TC), F32), jax.ShapeDtypeStruct((BR, BC), F32)),
        in_specs=[pl.BlockSpec(memory_space=pltpu.HBM)] * 8,
        out_specs=(pl.BlockSpec(memory_space=pltpu.HBM), vmem),
        scratch_shapes=[
            pltpu.VMEM((TR, TC), F32), pltpu.VMEM((TR, TC), jnp.int32), pltpu.VMEM((TR, TC), F32),
            pltpu.VMEM((BR, BC), F32), pltpu.VMEM((BR, BC), F32),
            pltpu.VMEM((1, S), jnp.int32), pltpu.VMEM((1, S), jnp.int32),
            pltpu.SMEM((1, C), jnp.int32), pltpu.SemaphoreType.DMA((9,)), pltpu.VMEM((TR, TC), F32),
            pltpu.VMEM((C, 8, per), F32), pltpu.VMEM((C, 8, per), F32),
            pltpu.VMEM((C, 1, per), F32), pltpu.VMEM((C, 1, per), F32),
            pltpu.VMEM((C, 1, per), F32), pltpu.VMEM((C, 1, per), F32),
            pltpu.VMEM((TC, S), BF16),
            pltpu.VMEM((S, TC), BF16),
            pltpu.VMEM(ext, F32),
            pltpu.VMEM((ITERS,) + ext, F32),
            pltpu.VMEM((ITERS - 1,) + ext, F32),
            pltpu.VMEM((TR, TC), F32),
            pltpu.VMEM((2, TR, LANES), F32),
            pltpu.VMEM((2, LANES, TR), F32),
            pltpu.VMEM((2, LANES, TR), F32),
            pltpu.VMEM((2, 8, TC), F32),
            pltpu.VMEM((2, 8, TC), F32),
            pltpu.VMEM((2, 4, 8, LANES), F32),
            pltpu.VMEM((16, LANES), F32), pltpu.VMEM((C - 1, 16, LANES), F32),
            pltpu.VMEM((16, LANES), F32), pltpu.VMEM((R - 1, 16, LANES), F32),
            pltpu.VMEM((BR, BC), F32),
            pltpu.VMEM((2, BC, BR), F32), pltpu.VMEM((2, 2, BC // GROUP, BR), F32),
            pltpu.VMEM((2, 8, BC), F32), pltpu.VMEM((2, 8, BC), F32),
            pltpu.VMEM((2, BC // GROUP, BR), F32), pltpu.VMEM((2, BC // GROUP, BR), F32),
            pltpu.SemaphoreType.DMA((copies,)),
            pltpu.SemaphoreType.DMA((copies,)),
        ],
        compiler_params=pltpu.CompilerParams(
            collective_id=0, has_side_effects=True, vmem_limit_bytes=60 * 1024 * 1024
        ),
    )(load_amp, load_mask, leak, coarse_leak, coarse_init, via_fine, via_coarse, via_count)


def solution(mesh):
    spec = P("row", "col")
    return jax.shard_map(
        functools.partial(per_device, mesh.shape["row"], mesh.shape["col"]),
        mesh=mesh, in_specs=(spec,) * 8, out_specs=(spec, spec), check_vma=False,
    )
```
